512 devices in a mesh: chan: 128 (over y, z, core), seg: 4 (over x).
Axes of the slice: x: 4, y: 8, z: 8, core: 2. Of those that a mesh axis runs over, the one named last changes fastest.
Arguments:
- recording: float32 [16384, 16384], P('chan', 'seg'), may hold values from -60 to 60
- filter_taps: float32 [64], replicated, may hold values from -0.75 to 0.75
- offsets: int32 [4], replicated, may hold values from -64 to 64, as said below
- loop_partner: int32 [128, 3], replicated, may hold values from 0 to 127, as said below
- loop_count: int32 [128], replicated, may hold values from 0 to 3, as said below
Outputs:
- near_corr: float32 [16384, 4, 256], P('chan', 'seg')
- loop_corr: float32 [128, 3, 128, 256], P('chan', None, 'seg')
The draws below stay inside these ranges and needn't reach their ends.
Inputs may be any that keep to these rules, and one draw needn't show every extreme that they name: 4 distinct nonzero offsets; both -64 and 64 are among them. `loop_partner`: slots at or beyond a block's loop_count are ignored. `loop_count`: some block uses all 3 slots.
All inputs are finite; a program needn't handle non-finite values.
Results may differ from the reference program's by a relative error of at most 0.004.
Values may be sent and summed in bfloat16 or wider, within the bound.
A program may use at most 64 MiB of HBM per device.

```python
import math
import jax
import jax.numpy as jnp
from jax import lax

C_DEV = 128
NOFF = 4
NFFT = 1024
LAGS = 256
TAPS = 64
DECIM = 4
SPAN = 64
MAXLB = 3
HALFBAND = 10
BINS = 512
CHANNELS = 16384
NBLK = 128
SEGS = 4
TIMES = 16384


def draw_recording(key, part):
    scale_key = jax.random.fold_in(key, 1)
    noise_key = jax.random.fold_in(key, 2)
    scales = jnp.exp(jax.random.uniform(scale_key, (CHANNELS, 1), jnp.float32, 0.0, math.log(10.0)))
    noise_part = jnp.clip(jax.random.normal(noise_key, (CHANNELS, TIMES), jnp.float32), -6.0, 6.0)
    return scales * noise_part


def draw_offsets(key, part):
    steps_up = jnp.arange(1, SPAN, dtype=jnp.int32)
    candidates = jnp.concatenate([steps_up, -steps_up])
    shuffled = jax.random.permutation(jax.random.fold_in(key, 5), candidates)
    chosen = jnp.concatenate([jnp.array([SPAN, -SPAN], jnp.int32), shuffled[:NOFF - 2]])
    return jax.random.permutation(jax.random.fold_in(key, 6), chosen).astype(jnp.int32)


def draw_loop_partner(key, part):
    jumps = jax.random.randint(jax.random.fold_in(key, 7), (NBLK, MAXLB), 0, NBLK - 1)
    own_ids = jnp.arange(NBLK, dtype=jnp.int32)[:, None]
    return ((own_ids + 1 + jumps) % NBLK).astype(jnp.int32)


def draw_loop_count(key, part):
    raw_counts = jax.random.randint(jax.random.fold_in(key, 11), (NBLK,), -3, MAXLB + 1)
    counts = jnp.maximum(raw_counts, 0)
    chosen = jax.random.randint(jax.random.fold_in(key, 12), (), 0, NBLK)
    counts = jnp.where(jnp.arange(NBLK, dtype=jnp.int32) == chosen, MAXLB, counts)
    return counts.astype(jnp.int32)


def noise(key, extent, width, limit, held_as=jnp.bfloat16):
    result = jax.random.normal(key, extent, jnp.float32) * width
    return jnp.minimum(jnp.maximum(result, -limit), limit).astype(held_as)


def setup_inputs(seed: int = 0) -> dict:
    key_list = jax.random.split(jax.random.key(seed), 6)
    recording = draw_recording(jax.random.fold_in(key_list[5], 71), 0)
    filter_taps = noise(key_list[1], (TAPS,), TAPS ** -0.5, 0.75, jnp.float32)
    offsets = draw_offsets(jax.random.fold_in(key_list[5], 71), 0)
    loop_partner = draw_loop_partner(jax.random.fold_in(key_list[5], 71), 0)
    loop_count = draw_loop_count(jax.random.fold_in(key_list[5], 71), 0)
    return dict(recording=recording, filter_taps=filter_taps, offsets=offsets, loop_partner=loop_partner, loop_count=loop_count)


WATER = 0.2

def decimate(extended, filter_taps):
    row_count = extended.shape[0]
    lead_rows = TAPS // DECIM
    grouped = extended.reshape(row_count, -1, DECIM)
    out_len = grouped.shape[1] - lead_rows
    summed = jnp.zeros((row_count, out_len), jnp.float32)
    for tap_group in range(lead_rows):
        tap_vec = filter_taps[DECIM * tap_group:DECIM * tap_group + DECIM][::-1]
        window = grouped[:, lead_rows - tap_group:lead_rows - tap_group + out_len, :]
        summed = summed + jnp.einsum('cmp,p->cm', window, tap_vec, precision=lax.Precision.HIGHEST)
    return summed

def forward_table(nblocks):
    bin_width = BINS // nblocks
    column = jnp.arange(2 * BINS, dtype=jnp.int32)
    block_id = column // (2 * bin_width)
    is_imag = column // bin_width % 2
    bin_index = block_id * bin_width + column % bin_width
    sample = jnp.arange(NFFT, dtype=jnp.int32)
    phase_idx = sample[:, None] * bin_index[None, :] % NFFT
    angles = phase_idx.astype(jnp.float32) * (2.0 * math.pi / NFFT)
    return jnp.where(is_imag[None, :] == 1, -jnp.sin(angles), jnp.cos(angles))

def inverse_table(nblocks, total_segs):
    bin_width = BINS // nblocks
    column = jnp.arange(2 * BINS, dtype=jnp.int32)
    block_id = column // (2 * bin_width)
    is_imag = column // bin_width % 2
    bin_index = block_id * bin_width + column % bin_width
    lag_index = jnp.arange(LAGS, dtype=jnp.int32) - LAGS // 2
    phase_idx = bin_index[:, None] * lag_index[None, :] % NFFT
    angles = phase_idx.astype(jnp.float32) * (2.0 * math.pi / NFFT)
    weights = jnp.where(bin_index == 0, 1.0, 2.0) / math.sqrt(2.0 * BINS * total_segs)
    return jnp.where(is_imag[:, None] == 1, -jnp.sin(angles), jnp.cos(angles)) * weights[:, None]

def band_matrix():
    bin_ids = jnp.arange(BINS, dtype=jnp.int32)
    inside = (jnp.abs(bin_ids[:, None] - bin_ids[None, :]) <= HALFBAND).astype(jnp.float32)
    return inside / lax.optimization_barrier(jnp.sum(inside, axis=0, keepdims=True))

def whiten(pieces, nblocks):
    row_count = pieces.shape[0]
    bin_width = BINS // nblocks
    spectrum = jnp.dot(pieces, forward_table(nblocks), precision=lax.Precision.HIGHEST, preferred_element_type=jnp.float32)
    parted = spectrum.reshape(row_count, nblocks, 2, bin_width)
    amplitude = jnp.sqrt(parted[:, :, 0] * parted[:, :, 0] + parted[:, :, 1] * parted[:, :, 1]).reshape(row_count, BINS)
    smoothed = jnp.dot(amplitude, band_matrix(), precision=lax.Precision.HIGHEST, preferred_element_type=jnp.float32)
    level_mean = lax.optimization_barrier(jnp.mean(amplitude, axis=1, keepdims=True))
    divisor = smoothed + WATER * level_mean + 1e-06
    whitened = parted / divisor.reshape(row_count, nblocks, 1, bin_width)
    return whitened.reshape(row_count, 2 * BINS).astype(jnp.bfloat16)

def cross(own, partner, nblocks, form):
    full_width = own.shape[-1]
    bin_width = full_width // (2 * nblocks)
    own_parts = own.astype(jnp.float32).reshape(own.shape[:-1] + (nblocks, 2, bin_width))
    far_parts = partner.astype(jnp.float32).reshape(partner.shape[:-1] + (nblocks, 2, bin_width))
    own_real = own_parts[..., 0, :]
    own_imag = own_parts[..., 1, :]
    far_real = far_parts[..., 0, :]
    far_imag = far_parts[..., 1, :]
    high = lax.Precision.HIGHEST
    real_part = jnp.einsum(form, own_real, far_real, precision=high) + jnp.einsum(form, own_imag, far_imag, precision=high)
    imag_part = jnp.einsum(form, own_imag, far_real, precision=high) - jnp.einsum(form, own_real, far_imag, precision=high)
    joined = jnp.stack([real_part, imag_part], axis=-2)
    return joined.reshape(joined.shape[:-3] + (full_width,))

def to_lags(pair_spec, inverse):
    lead_shape = pair_spec.shape[:-1]
    lag_rows = jnp.dot(pair_spec.reshape(-1, pair_spec.shape[-1]), inverse, precision=lax.Precision.HIGHEST, preferred_element_type=jnp.float32)
    return lag_rows.reshape(lead_shape + (LAGS,))

def reference(recording, filter_taps, offsets, loop_partner, loop_count):
    chan_blocks = recording.reshape(NBLK, C_DEV, TIMES)

    def block_spectra(block_rec):
        padded = jnp.concatenate([jnp.zeros((C_DEV, TAPS), jnp.float32), block_rec], axis=1)
        decimated = decimate(padded, filter_taps)
        pieces = decimated.reshape(C_DEV, SEGS, NFFT)
        pieces = pieces - lax.optimization_barrier(jnp.mean(pieces, axis=2, keepdims=True))
        return whiten(pieces.reshape(C_DEV * SEGS, NFFT), 1).reshape(C_DEV, SEGS, 2 * BINS)
    whitened = lax.map(block_spectra, chan_blocks)
    flat_white = whitened.reshape(CHANNELS, SEGS, 2 * BINS)
    inverse = inverse_table(1, SEGS)

    def near_block(block_id):
        channel_ids = block_id * C_DEV + jnp.arange(C_DEV, dtype=jnp.int32)
        partner_ids = (channel_ids[None, :] + offsets[:, None]) % CHANNELS
        pair_spec = cross(flat_white[channel_ids], flat_white[partner_ids], 1, 'csnt,pcsnt->cpnt')
        return to_lags(pair_spec, inverse)
    block_ids = jnp.arange(NBLK, dtype=jnp.int32)
    near_corr = lax.map(near_block, block_ids).reshape(CHANNELS, NOFF, LAGS)

    def loop_block(block_id):
        partner = whitened[loop_partner[block_id]][:, ::-1]
        live_slots = (jnp.arange(MAXLB, dtype=jnp.int32) < loop_count[block_id]).astype(jnp.float32)
        pair_spec = cross(whitened[block_id], partner, 1, 'csnt,kcsnt->kcnt') * live_slots[:, None, None]
        return to_lags(pair_spec, inverse)
    loop_corr = lax.map(loop_block, block_ids)
    return (near_corr, loop_corr)
```

```python
import math

import jax
import jax.numpy as jnp
import numpy as np
from jax import lax
from jax.experimental import pallas as pl
from jax.experimental.pallas import tpu as pltpu
from jax.sharding import PartitionSpec as P

C = 128
NOFF = 4
NFFT = 1024
LAGS = 256
TAPS = 64
DECIM = 4
HALFBAND = 10
BINS = 512
MAXLB = 3
SEGS = 4
WATER = 0.2
X, Y, ZC = 4, 8, 16
XY = X * Y
RIM = 128
QB = 128
WIN = DECIM * QB + RIM
NB = NFFT // QB
MESH = pl.DeviceIdType.MESH
BF = jnp.bfloat16
F32 = jnp.float32


def split_np(a):
    hi = a.astype(np.float32).astype(jnp.bfloat16)
    lo = (a - hi.astype(np.float64)).astype(np.float32).astype(jnp.bfloat16)
    return hi, lo


def bin_order():
    p = np.arange(BINS)
    return np.where(p < BINS // 2, 2 * p, 2 * (p - BINS // 2) + 1)


def forward_tables():
    sample = np.arange(NFFT // 2)
    out = []
    for odd in range(2):
        bins = 2 * np.arange(BINS // 2) + odd
        angle = 2.0 * np.pi * (bins[:, None] * sample[None, :] % NFFT) / NFFT
        real = np.cos(angle) * (bins[:, None] > 0)
        out.extend(split_np(np.concatenate([real, -np.sin(angle)], axis=0)))
    return np.stack(out)


def lag_tables():
    bins = bin_order()
    lag = np.arange(LAGS) - LAGS // 2
    angle = 2.0 * np.pi * (bins[None, :] * lag[:, None] % NFFT) / NFFT
    weight = np.where(bins == 0, 1.0, 2.0) / math.sqrt(2.0 * BINS * SEGS)
    both = np.concatenate([np.cos(angle) * weight, -np.sin(angle) * weight], axis=1)
    return np.stack(split_np(both))


def dot(a, b):
    return jnp.dot(a, b, preferred_element_type=F32)


def dot_nt(a, b):
    return lax.dot_general(a, b, (((1,), (1,)), ((), ())), preferred_element_type=F32)


def halves(a):
    hi = a.astype(BF)
    return hi, (a - hi.astype(F32)).astype(BF)


def iota(shape, dim):
    return lax.broadcasted_iota(jnp.int32, shape, dim)


def where_am_i():
    chan = lax.axis_index("chan")
    return lax.axis_index("seg"), chan // ZC, lax.rem(chan, ZC)


def kernel(
    off_ref, rec_hbm, taps_ref, part_ref, count_ref, fwd_hbm, lag_hbm,
    near_out, loop_out,
    raw, rec, dec, fwd, lagt, perm, permt, band, rim_send, rim_recv,
    spec, uv, white_a, white_b, halo_send, halo_recv,
    a1, a2, a3, b1, b2, b3, wr, wi, a4, a5, b4, b5, near_part, near_send, near_recv, back_a, back_b,
    local_sem, rim_sem, halo_sem, near_sem, ssem, rsem,
):
    x, y, zc = where_am_i()
    chan = lax.axis_index("chan")

    def zc_dev(i):
        return (y * ZC + i, x)

    def xy_dev(i):
        return (lax.rem(i, Y) * ZC + zc, i // Y)

    me_xy = x * Y + y
    before = (lax.rem(chan + C - 1, C), x)
    after = (lax.rem(chan + 1, C), x)

    loads = []
    order = [NB - 1] + list(range(NB - 1))
    for n, b in enumerate(order):
        cols = pl.ds(b * DECIM * QB, DECIM * QB)
        loads.append(pltpu.make_async_copy(rec_hbm.at[:, cols], raw.at[:, cols], local_sem.at[n]))
    load_fwd = pltpu.make_async_copy(fwd_hbm, fwd, local_sem.at[NB])
    load_lag = pltpu.make_async_copy(lag_hbm, lagt, local_sem.at[NB + 1])
    for c in loads:
        c.start()
    load_fwd.start()
    load_lag.start()

    barrier = pltpu.get_barrier_semaphore()

    def signal_zc(i, _):
        pl.semaphore_signal(barrier, inc=1, device_id=zc_dev(lax.rem(zc + i, ZC)), device_id_type=MESH)
        return 0

    def signal_xy(i, _):
        pl.semaphore_signal(barrier, inc=1, device_id=xy_dev(lax.rem(me_xy + i, XY)), device_id_type=MESH)
        return 0

    lax.fori_loop(1, ZC, signal_zc, 0)
    lax.fori_loop(1, XY, signal_xy, 0)
    pl.semaphore_signal(barrier, inc=1, device_id=before, device_id_type=MESH)
    pl.semaphore_signal(barrier, inc=1, device_id=after, device_id_type=MESH)

    r = iota((BINS, BINS), 0)
    c = iota((BINS, BINS), 1)
    perm[...] = jnp.where(c == lax.rem(r, ZC) * XY + r // ZC, 1.0, 0.0).astype(BF)
    permt[...] = jnp.where(c == lax.rem(r, XY) * ZC + r // XY, 1.0, 0.0).astype(BF)
    half = BINS // 2
    fr = jnp.where(r < half, 2 * r, 2 * (r - half) + 1)
    fc = jnp.where(c < half, 2 * c, 2 * (c - half) + 1)
    band[...] = jnp.where(jnp.abs(fr - fc) <= HALFBAND, 1.0, 0.0).astype(BF)

    place = (iota((TAPS, WIN), 1) == 67 + TAPS - iota((TAPS, WIN), 0))
    place = jnp.where(place, 1.0, 0.0).astype(BF)
    t_hi, t_lo = halves(jnp.broadcast_to(taps_ref[...], (8, TAPS)))
    row_hi = jnp.broadcast_to(dot(t_hi, place)[0:1], (QB, WIN))
    row_lo = jnp.broadcast_to(dot(t_lo, place)[0:1], (QB, WIN))
    tab_hi = pltpu.roll(row_hi, 0, 1, stride=DECIM, stride_axis=0).astype(BF)
    tab_lo = pltpu.roll(row_lo, 0, 1, stride=DECIM, stride_axis=0).astype(BF)

    def take(n):
        b = order[n]
        loads[n].wait()
        cols = pl.ds(b * DECIM * QB, DECIM * QB)
        hi, lo = halves(raw[:, cols])
        to = pl.ds(RIM + b * DECIM * QB, DECIM * QB)
        rec[0:C, to] = hi
        rec[C : 2 * C, to] = lo

    def decimate(b):
        win = pl.ds(b * DECIM * QB, WIN)
        both = dot_nt(tab_hi, rec[:, win])
        out = both[:, :C] + both[:, C:] + dot_nt(tab_lo, rec[0:C, win])
        dec[b * QB : (b + 1) * QB, :] = out

    take(0)
    rim_send[...] = raw[:, NFFT * DECIM - RIM :].astype(BF)
    for n in range(1, NB):
        take(n)
        if order[n] > 0:
            decimate(order[n])
    decimate(NB - 1)

    pl.semaphore_wait(barrier, ZC - 1 + XY - 1 + 2)
    rim = pltpu.make_async_remote_copy(
        rim_send, rim_recv, rim_sem.at[0], rim_sem.at[1],
        device_id=(chan, lax.rem(x + 1, X)), device_id_type=MESH,
    )
    rim.start()

    level = jnp.sum(dec[QB:, :], axis=0, keepdims=True) * (1.0 / (NFFT - QB))

    def fold(lo_row, hi_row):
        low = dec[lo_row:hi_row, :] - level
        high = dec[lo_row + NFFT // 2 : hi_row + NFFT // 2, :] - level
        for k, v in enumerate((low + high, low - high)):
            hi, lo = halves(v)
            uv[k, lo_row:hi_row, 0:C] = hi
            uv[k, lo_row:hi_row, C : 2 * C] = lo

    def transform(lo_row, hi_row):
        outs = []
        for k in range(2):
            v = uv[k, lo_row:hi_row, :]
            both = dot(fwd[2 * k, :, lo_row:hi_row], v)
            outs.append(both[:, :C] + both[:, C:] + dot(fwd[2 * k + 1, :, lo_row:hi_row], v[:, :C]))
        return outs

    fold(QB, NFFT // 2)
    load_fwd.wait()
    for k, s in enumerate(transform(QB, NFFT // 2)):
        spec[k] = s

    rim.wait()
    inside = (iota((C, RIM), 1) >= RIM - TAPS) & (x > 0)
    rec[0:C, 0:RIM] = jnp.where(inside, rim_recv[...].astype(F32), 0.0).astype(BF)
    rec[C : 2 * C, 0:RIM] = jnp.zeros((C, RIM), BF)
    decimate(0)
    fold(0, QB)
    for k, s in enumerate(transform(0, QB)):
        spec[k] = spec[k] + s

    real = jnp.concatenate([spec[0, :half, :], spec[1, :half, :]], axis=0)
    imag = jnp.concatenate([spec[0, half:, :], spec[1, half:, :]], axis=0)
    amp = jnp.sqrt(real * real + imag * imag)
    amp_hi, amp_lo = halves(amp)
    near_sum = dot(band[...], amp_hi) + dot(band[...], amp_lo)
    rows = iota((BINS, C), 0)
    f = jnp.where(rows < half, 2 * rows, 2 * (rows - half) + 1)
    width = jnp.minimum(f, HALFBAND) + jnp.minimum(BINS - 1 - f, HALFBAND) + 1
    mean_amp = jnp.sum(amp, axis=0, keepdims=True) * (1.0 / BINS)
    divisor = near_sum / width.astype(F32) + WATER * mean_amp + 1e-06
    wre = (real / divisor).astype(BF)
    wim = (imag / divisor).astype(BF)
    white_a[...] = wre
    white_b[...] = dot(perm[...], wim).astype(BF)

    def send_zc(src, dst, k):
        def body(i, _):
            d = lax.rem(zc + i, ZC)
            pltpu.make_async_remote_copy(
                src.at[pl.ds(d * XY, XY)], dst.at[pl.ds(zc * XY, XY)], ssem.at[k], rsem.at[k],
                device_id=zc_dev(d), device_id_type=MESH,
            ).start()
            return 0

        lax.fori_loop(1, ZC, body, 0)
        mine = pl.ds(pl.multiple_of(zc * XY, XY), XY)
        dst[mine, :] = src[mine, :]

    def send_xy(src, dst, k):
        def body(i, _):
            d = lax.rem(me_xy + i, XY)
            pltpu.make_async_remote_copy(
                src.at[pl.ds(d * ZC, ZC)], dst.at[pl.ds(me_xy * ZC, ZC)], ssem.at[k], rsem.at[k],
                device_id=xy_dev(d), device_id_type=MESH,
            ).start()
            return 0

        lax.fori_loop(1, XY, body, 0)
        mine = pl.ds(pl.multiple_of(me_xy * ZC, ZC), ZC)
        dst[mine, :] = src[mine, :]

    def done(ref, sems, k, count):
        part = ref.at[pl.ds(0, count)]
        pltpu.make_async_copy(part, part, sems.at[k]).wait()

    zc_rows = (ZC - 1) * XY
    xy_rows = (XY - 1) * ZC

    send_zc(white_a, a1, 0)
    send_xy(white_b, b1, 1)

    lane = iota((BINS, C), 1)
    left = lane < 64
    wre = wre.astype(F32)
    wim = wim.astype(F32)
    halo_send[0] = jnp.where(left, wre, pltpu.roll(wim, 64, 1)).astype(BF)
    halo_send[1] = jnp.where(left, pltpu.roll(wre, 64, 1), wim).astype(BF)
    to_before = pltpu.make_async_remote_copy(
        halo_send.at[0], halo_recv.at[0], halo_sem.at[0], halo_sem.at[1],
        device_id=before, device_id_type=MESH,
    )
    to_after = pltpu.make_async_remote_copy(
        halo_send.at[1], halo_recv.at[1], halo_sem.at[2], halo_sem.at[3],
        device_id=after, device_id_type=MESH,
    )
    to_before.start()
    to_after.start()
    to_before.wait()
    to_after.wait()
    load_lag.wait()

    def near(o, _):
        off = off_ref[o]
        own_r = white_a[...].astype(F32)
        own_i = wim
        nxt = halo_recv[0].astype(F32)
        prv = halo_recv[1].astype(F32)
        far_r = jnp.where(left, nxt, pltpu.roll(prv, 64, 1))
        far_i = jnp.where(left, pltpu.roll(nxt, 64, 1), prv)
        src = lane - off
        keep = (src >= 0) & (src < C)
        turn = lax.rem(C - off, C)
        pr = pltpu.roll(jnp.where(keep, own_r, far_r), turn, 1)
        pi = pltpu.roll(jnp.where(keep, own_i, far_i), turn, 1)
        sr = own_r * pr + own_i * pi
        si = own_i * pr - own_r * pi
        out = jnp.zeros((LAGS, C), F32)
        for k, s in enumerate((sr, si)):
            hi, lo = halves(s)
            cols = slice(k * BINS, (k + 1) * BINS)
            out = out + dot(lagt[0, :, cols], hi) + dot(lagt[0, :, cols], lo) + dot(lagt[1, :, cols], hi)
        near_part[o] = out
        near_send[o] = out.astype(BF)
        return 0

    lax.fori_loop(0, 2, near, 0)

    done(a1, rsem, 0, zc_rows)
    a2[...] = dot(perm[...], a1[...]).astype(BF)
    send_xy(a2, wr, 2)
    done(b1, rsem, 1, xy_rows)
    b2[...] = dot(permt[...], b1[...]).astype(BF)
    send_zc(b2, b3, 3)

    lax.fori_loop(2, NOFF, near, 0)

    def near_to(i, k):
        d = lax.rem(x + i, X)
        return pltpu.make_async_remote_copy(
            near_send.at[d], near_recv.at[i - 1], near_sem.at[0], near_sem.at[1],
            device_id=(chan, d), device_id_type=MESH,
        )

    for i in range(1, X):
        near_to(i, 0).start()

    lane_b = iota((C, C), 1)
    row_b = iota((C, C), 0)
    flip = jnp.where(lane_b + row_b == C - 1, 1.0, 0.0).astype(BF)
    picks = []
    for k in range(MAXLB):
        line = jnp.where(count_ref[...] > k, part_ref[k : k + 1, :], -1).astype(F32)
        column = jnp.sum(jnp.where(lane_b == row_b, jnp.broadcast_to(line, (C, C)), 0.0), axis=1, keepdims=True)
        picks.append(jnp.where(column == lane_b.astype(F32), 1.0, 0.0).astype(BF))
    pick = jnp.concatenate(picks, axis=0)

    done(wr, rsem, 2, xy_rows)
    done(b3, rsem, 3, zc_rows)
    wi[...] = dot(perm[...], b3[...]).astype(BF)

    loop_r = [jnp.zeros((C, C), F32) for _ in range(MAXLB)]
    loop_i = [jnp.zeros((C, C), F32) for _ in range(MAXLB)]
    for s in range(SEGS):
        own_r = wr[s * C : (s + 1) * C, :]
        own_i = wi[s * C : (s + 1) * C, :]
        far_r = dot(pick, dot(own_r, flip).astype(BF))
        far_i = dot(pick, dot(own_i, flip).astype(BF))
        own_r = own_r.astype(F32)
        own_i = own_i.astype(F32)
        for k in range(MAXLB):
            pr = far_r[k * C : (k + 1) * C, :]
            pi = far_i[k * C : (k + 1) * C, :]
            loop_r[k] = loop_r[k] + own_r * pr + own_i * pi
            loop_i[k] = loop_i[k] + own_i * pr - own_r * pi

    def gather_lanes(parts, q):
        out = jnp.zeros((C, C), F32)
        for j, p in enumerate(parts):
            turned = p if j == q else pltpu.roll(p, 32 * ((j - q) % 4), 1)
            out = jnp.where((lane_b >= 32 * j) & (lane_b < 32 * (j + 1)), turned, out)
        return out.astype(BF)

    for q in range(X):
        rows = slice(q * C, (q + 1) * C)
        back_a[rows, :] = gather_lanes([loop_r[0], loop_i[0], loop_r[1], loop_i[1]], q)
        back_b[rows, :] = gather_lanes([loop_r[2], loop_i[2]], q)

    done(a2, ssem, 2, xy_rows)
    done(b2, ssem, 3, zc_rows)
    done(white_a, ssem, 0, zc_rows)
    done(white_b, ssem, 1, xy_rows)
    a3[...] = dot(permt[...], back_a[...]).astype(BF)
    send_zc(a3, a4, 4)
    send_xy(back_b, b4, 5)

    three = near_recv.at[pl.ds(0, X - 1)]
    pltpu.make_async_copy(three, three, near_sem.at[1]).wait()
    total = near_part[x]
    for i in range(X - 1):
        total = total + near_recv[i].astype(F32)
    near_out[...] = jnp.transpose(total)

    done(a4, rsem, 4, zc_rows)
    a2[...] = dot(perm[...], a4[...]).astype(BF)
    send_xy(a2, a5, 6)
    done(b4, rsem, 5, xy_rows)
    b2[...] = dot(permt[...], b4[...]).astype(BF)
    send_zc(b2, b5, 7)

    done(a5, rsem, 6, xy_rows)
    got_a = dot(permt[...], a5[...]).astype(BF)
    lag_r = dot(lagt[0, :, :BINS], got_a) + dot(lagt[1, :, :BINS], got_a)
    lag_i = dot(lagt[0, :, BINS:], got_a) + dot(lagt[1, :, BINS:], got_a)
    lag_r = jnp.transpose(lag_r)
    lag_i = jnp.transpose(lag_i)
    loop_out[0] = lag_r[0:32] + lag_i[32:64]
    loop_out[1] = lag_r[64:96] + lag_i[96:128]
    done(b5, rsem, 7, zc_rows)
    got_b = b5[...]
    lag_r = dot(lagt[0, :, :BINS], got_b) + dot(lagt[1, :, :BINS], got_b)
    lag_i = dot(lagt[0, :, BINS:], got_b) + dot(lagt[1, :, BINS:], got_b)
    lag_r = jnp.transpose(lag_r)
    lag_i = jnp.transpose(lag_i)
    loop_out[2] = lag_r[0:32] + lag_i[32:64]

    pltpu.make_async_copy(three, three, near_sem.at[0]).wait()
    done(a3, ssem, 4, zc_rows)
    done(back_b, ssem, 5, xy_rows)
    done(a2, ssem, 6, xy_rows)
    done(b2, ssem, 7, zc_rows)


def body(recording, filter_taps, offsets, loop_partner, loop_count):
    fwd = jnp.asarray(forward_tables())
    lagt = jnp.asarray(lag_tables())
    vmem = pl.BlockSpec(memory_space=pltpu.VMEM)
    hbm = pl.BlockSpec(memory_space=pl.ANY)
    smem = pl.BlockSpec(memory_space=pltpu.SMEM)
    rows = pltpu.VMEM((BINS, C), BF)
    dma = pltpu.SemaphoreType.DMA
    near, loop = pl.pallas_call(
        kernel,
        out_shape=(
            jax.ShapeDtypeStruct((C, LAGS), F32),
            jax.ShapeDtypeStruct((MAXLB, C // X, LAGS), F32),
        ),
        in_specs=[smem, hbm, vmem, vmem, vmem, hbm, hbm],
        out_specs=(vmem, vmem),
        scratch_shapes=[
            pltpu.VMEM((C, NFFT * DECIM), F32),
            pltpu.VMEM((2 * C, RIM + NFFT * DECIM), BF),
            pltpu.VMEM((NFFT, C), F32),
            pltpu.VMEM((4, BINS, NFFT // 2), BF),
            pltpu.VMEM((2, LAGS, 2 * BINS), BF),
            pltpu.VMEM((BINS, BINS), BF),
            pltpu.VMEM((BINS, BINS), BF),
            pltpu.VMEM((BINS, BINS), BF),
            pltpu.VMEM((C, RIM), BF),
            pltpu.VMEM((C, RIM), BF),
            pltpu.VMEM((2, BINS, C), F32),
            pltpu.VMEM((2, NFFT // 2, 2 * C), BF),
            rows, rows,
            pltpu.VMEM((2, BINS, C), BF),
            pltpu.VMEM((2, BINS, C), BF),
            rows, rows, rows, rows, rows, rows, rows, rows, rows, rows, rows, rows,
            pltpu.VMEM((NOFF, LAGS, C), F32),
            pltpu.VMEM((NOFF, LAGS, C), BF),
            pltpu.VMEM((X - 1, LAGS, C), BF),
            rows, rows,
            dma((NB + 2,)), dma((2,)), dma((4,)), dma((2,)), dma((8,)), dma((8,)),
        ],
        compiler_params=pltpu.CompilerParams(collective_id=0, has_side_effects=True),
    )(
        offsets, recording, filter_taps.reshape(1, TAPS), loop_partner.T,
        loop_count.reshape(1, C), fwd, lagt,
    )
    return near[:, None, :], loop[None]


def solution(mesh):
    in_specs = (P("chan", "seg"), P(), P(), P(), P())
    out_specs = (P("chan", "seg", None), P("chan", None, "seg", None))
    return jax.shard_map(body, mesh=mesh, in_specs=in_specs, out_specs=out_specs, check_vma=False)
```

```python
import math

import jax
import jax.numpy as jnp
import numpy as np
from jax import lax
from jax.experimental import pallas as pl
from jax.experimental.pallas import tpu as pltpu
from jax.sharding import PartitionSpec as P

C = 128
NOFF = 4
NFFT = 1024
LAGS = 256
TAPS = 64
DECIM = 4
HALFBAND = 10
BINS = 512
MAXLB = 3
SEGS = 4
WATER = 0.2
X, Y, ZC = 4, 8, 16
XY = X * Y
RIM = 128
QB = 128
WIN = DECIM * QB + RIM
NB = NFFT // QB
MESH = pl.DeviceIdType.MESH
BF = jnp.bfloat16
F32 = jnp.float32


def split_np(a):
    hi = a.astype(np.float32).astype(jnp.bfloat16)
    lo = (a - hi.astype(np.float64)).astype(np.float32).astype(jnp.bfloat16)
    return hi, lo


def bin_order():
    p = np.arange(BINS)
    return np.where(p < BINS // 2, 2 * p, 2 * (p - BINS // 2) + 1)


def forward_tables():
    sample = np.arange(NFFT // 2)
    out = []
    for odd in range(2):
        bins = 2 * np.arange(BINS // 2) + odd
        angle = 2.0 * np.pi * (bins[:, None] * sample[None, :] % NFFT) / NFFT
        real = np.cos(angle) * (bins[:, None] > 0)
        out.extend(split_np(np.concatenate([real, -np.sin(angle)], axis=0)))
    return np.stack(out)


def lag_tables():
    bins = bin_order()
    lag = np.arange(LAGS) - LAGS // 2
    angle = 2.0 * np.pi * (bins[None, :] * lag[:, None] % NFFT) / NFFT
    weight = np.where(bins == 0, 1.0, 2.0) / math.sqrt(2.0 * BINS * SEGS)
    both = np.concatenate([np.cos(angle) * weight, -np.sin(angle) * weight], axis=1)
    return np.stack(split_np(both))


def dot(a, b):
    return jnp.dot(a, b, preferred_element_type=F32)


def dot_nt(a, b):
    return lax.dot_general(a, b, (((1,), (1,)), ((), ())), preferred_element_type=F32)


def halves(a):
    hi = a.astype(BF)
    return hi, (a - hi.astype(F32)).astype(BF)


def iota(shape, dim):
    return lax.broadcasted_iota(jnp.int32, shape, dim)


def wrap(v, n):
    v = jnp.where(v >= n, v - n, v)
    return jnp.where(v < 0, v + n, v)


def where_am_i():
    chan = lax.axis_index("chan")
    return lax.axis_index("seg"), chan // ZC, lax.rem(chan, ZC)


def kernel(
    off_hbm, rec_hbm, taps_hbm, part_hbm, count_hbm, fwd_hbm, lag_hbm,
    near_out, loop_out,
    off_ref, taps_ref, part_ref, count_ref,
    raw, rec, dec, fwd, lagt, perm, permt, band, rim_send, rim_recv,
    spec, uv, white_a, white_b, halo_send, halo_recv,
    a1, a2, a3, b1, b2, b3, wr, wi, a4, a5, b4, b5, near_part, near_send, near_recv, back_a, back_b,
    local_sem, small_sem, rim_sem, halo_sem, near_sem, ssem, rsem,
):
    x, y, zc = where_am_i()
    chan = lax.axis_index("chan")

    def zc_dev(d):
        return (y * ZC + d, x)

    def xy_dev(x2, y2):
        return (y2 * ZC + zc, x2)

    me_xy = x * Y + y

    xs = [wrap(x + dx, X) for dx in range(X)]

    def each_zc(do):
        do(wrap(zc + ZC // 2, ZC))

        def pair(i, _):
            do(wrap(zc + (ZC // 2 - i), ZC))
            do(wrap(zc - (ZC // 2 - i), ZC))
            return 0

        lax.fori_loop(1, ZC // 2, pair, 0)

    def each_xy(do):
        def row(y2, dxs):
            for dx in dxs:
                do(xs[dx], y2)

        row(wrap(y + Y // 2, Y), (2, 1, 3, 0))

        def pair(i, _):
            row(wrap(y + (Y // 2 - i), Y), (2, 1, 3, 0))
            row(wrap(y - (Y // 2 - i), Y), (2, 1, 3, 0))
            return 0

        lax.fori_loop(1, Y // 2, pair, 0)
        row(y, (2, 1, 3))

    before = (lax.rem(chan + C - 1, C), x)
    after = (lax.rem(chan + 1, C), x)

    loads = []
    order = [NB - 1] + list(range(NB - 1))
    for n, b in enumerate(order):
        cols = pl.ds(b * DECIM * QB, DECIM * QB)
        loads.append(pltpu.make_async_copy(rec_hbm.at[:, cols], raw.at[:, cols], local_sem.at[n]))
    load_fwd = pltpu.make_async_copy(fwd_hbm, fwd, local_sem.at[NB])
    load_lag = pltpu.make_async_copy(lag_hbm, lagt, local_sem.at[NB + 1])
    small = [
        pltpu.make_async_copy(src, dst, small_sem.at[n])
        for n, (src, dst) in enumerate((
            (taps_hbm, taps_ref), (off_hbm, off_ref), (part_hbm, part_ref), (count_hbm, count_ref),
        ))
    ]
    for c in small + loads:
        c.start()
    load_fwd.start()
    load_lag.start()

    barrier = pltpu.get_barrier_semaphore()

    def signal(device):
        pl.semaphore_signal(barrier, inc=1, device_id=device, device_id_type=MESH)

    each_zc(lambda d: signal(zc_dev(d)))
    each_xy(lambda x2, y2: signal(xy_dev(x2, y2)))
    signal(before)
    signal(after)

    r = iota((BINS, BINS), 0)
    c = iota((BINS, BINS), 1)
    perm[...] = jnp.where(c == lax.rem(r, ZC) * XY + r // ZC, 1.0, 0.0).astype(BF)
    permt[...] = jnp.where(c == lax.rem(r, XY) * ZC + r // XY, 1.0, 0.0).astype(BF)
    half = BINS // 2
    fr = jnp.where(r < half, 2 * r, 2 * (r - half) + 1)
    fc = jnp.where(c < half, 2 * c, 2 * (c - half) + 1)
    band[...] = jnp.where(jnp.abs(fr - fc) <= HALFBAND, 1.0, 0.0).astype(BF)

    place = (iota((TAPS, WIN), 1) == 67 + TAPS - iota((TAPS, WIN), 0))
    place = jnp.where(place, 1.0, 0.0).astype(BF)
    small[0].wait()
    t_hi, t_lo = halves(jnp.broadcast_to(taps_ref[...], (8, TAPS)))
    row_hi = jnp.broadcast_to(dot(t_hi, place)[0:1], (QB, WIN))
    row_lo = jnp.broadcast_to(dot(t_lo, place)[0:1], (QB, WIN))
    tab_hi = pltpu.roll(row_hi, 0, 1, stride=DECIM, stride_axis=0).astype(BF)
    tab_lo = pltpu.roll(row_lo, 0, 1, stride=DECIM, stride_axis=0).astype(BF)

    def take(n):
        b = order[n]
        loads[n].wait()
        cols = pl.ds(b * DECIM * QB, DECIM * QB)
        hi, lo = halves(raw[:, cols])
        to = pl.ds(RIM + b * DECIM * QB, DECIM * QB)
        rec[0:C, to] = hi
        rec[C : 2 * C, to] = lo

    def decimate(b):
        win = pl.ds(b * DECIM * QB, WIN)
        both = dot_nt(tab_hi, rec[:, win])
        out = both[:, :C] + both[:, C:] + dot_nt(tab_lo, rec[0:C, win])
        dec[b * QB : (b + 1) * QB, :] = out

    take(0)
    rim_send[...] = raw[:, NFFT * DECIM - RIM :].astype(BF)
    for n in range(1, NB):
        take(n)
        if order[n] > 0:
            decimate(order[n])
    decimate(NB - 1)

    pl.semaphore_wait(barrier, ZC - 1 + XY - 1 + 2)
    rim = pltpu.make_async_remote_copy(
        rim_send, rim_recv, rim_sem.at[0], rim_sem.at[1],
        device_id=(chan, lax.rem(x + 1, X)), device_id_type=MESH,
    )
    rim.start()

    level = jnp.sum(dec[QB:, :], axis=0, keepdims=True) * (1.0 / (NFFT - QB))

    def fold(lo_row, hi_row):
        low = dec[lo_row:hi_row, :] - level
        high = dec[lo_row + NFFT // 2 : hi_row + NFFT // 2, :] - level
        for k, v in enumerate((low + high, low - high)):
            hi, lo = halves(v)
            uv[k, lo_row:hi_row, 0:C] = hi
            uv[k, lo_row:hi_row, C : 2 * C] = lo

    def transform(lo_row, hi_row):
        outs = []
        for k in range(2):
            v = uv[k, lo_row:hi_row, :]
            both = dot(fwd[2 * k, :, lo_row:hi_row], v)
            outs.append(both[:, :C] + both[:, C:] + dot(fwd[2 * k + 1, :, lo_row:hi_row], v[:, :C]))
        return outs

    fold(QB, NFFT // 2)
    load_fwd.wait()
    for k, s in enumerate(transform(QB, NFFT // 2)):
        spec[k] = s

    rim.wait()
    inside = (iota((C, RIM), 1) >= RIM - TAPS) & (x > 0)
    rec[0:C, 0:RIM] = jnp.where(inside, rim_recv[...].astype(F32), 0.0).astype(BF)
    rec[C : 2 * C, 0:RIM] = jnp.zeros((C, RIM), BF)
    decimate(0)
    fold(0, QB)
    for k, s in enumerate(transform(0, QB)):
        spec[k] = spec[k] + s

    real = jnp.concatenate([spec[0, :half, :], spec[1, :half, :]], axis=0)
    imag = jnp.concatenate([spec[0, half:, :], spec[1, half:, :]], axis=0)
    amp = jnp.sqrt(real * real + imag * imag)
    amp_hi, amp_lo = halves(amp)
    near_sum = dot(band[...], amp_hi) + dot(band[...], amp_lo)
    rows = iota((BINS, C), 0)
    f = jnp.where(rows < half, 2 * rows, 2 * (rows - half) + 1)
    width = jnp.minimum(f, HALFBAND) + jnp.minimum(BINS - 1 - f, HALFBAND) + 1
    mean_amp = jnp.sum(amp, axis=0, keepdims=True) * (1.0 / BINS)
    divisor = near_sum / width.astype(F32) + WATER * mean_amp + 1e-06
    wre = (real / divisor).astype(BF)
    wim = (imag / divisor).astype(BF)
    white_a[...] = wre
    white_b[...] = dot(perm[...], wim).astype(BF)

    def send_zc(src, dst, k):
        mine = pl.ds(pl.multiple_of(zc * XY, XY), XY)

        def one(d):
            pltpu.make_async_remote_copy(
                src.at[pl.ds(pl.multiple_of(d * XY, XY), XY)], dst.at[mine], ssem.at[k], rsem.at[k],
                device_id=zc_dev(d), device_id_type=MESH,
            ).start()

        each_zc(one)
        dst[mine, :] = src[mine, :]

    def send_xy(src, dst, k):
        mine = pl.ds(pl.multiple_of(me_xy * ZC, ZC), ZC)

        def one(x2, y2):
            pltpu.make_async_remote_copy(
                src.at[pl.ds(pl.multiple_of((x2 * Y + y2) * ZC, ZC), ZC)], dst.at[mine], ssem.at[k], rsem.at[k],
                device_id=xy_dev(x2, y2), device_id_type=MESH,
            ).start()

        each_xy(one)
        dst[mine, :] = src[mine, :]

    def done(ref, sems, k, count):
        part = ref.at[pl.ds(0, count)]
        pltpu.make_async_copy(part, part, sems.at[k]).wait()

    zc_rows = (ZC - 1) * XY
    xy_rows = (XY - 1) * ZC

    send_zc(white_a, a1, 0)
    send_xy(white_b, b1, 1)

    lane = iota((BINS, C), 1)
    left = lane < 64
    wre = wre.astype(F32)
    wim = wim.astype(F32)
    halo_send[0] = jnp.where(left, wre, pltpu.roll(wim, 64, 1)).astype(BF)
    halo_send[1] = jnp.where(left, pltpu.roll(wre, 64, 1), wim).astype(BF)
    to_before = pltpu.make_async_remote_copy(
        halo_send.at[0], halo_recv.at[0], halo_sem.at[0], halo_sem.at[1],
        device_id=before, device_id_type=MESH,
    )
    to_after = pltpu.make_async_remote_copy(
        halo_send.at[1], halo_recv.at[1], halo_sem.at[2], halo_sem.at[3],
        device_id=after, device_id_type=MESH,
    )
    to_before.start()
    to_after.start()
    to_before.wait()
    to_after.wait()
    load_lag.wait()
    for c in small[1:]:
        c.wait()

    def near(o, _):
        off = off_ref[o]
        own_r = white_a[...].astype(F32)
        own_i = wim
        nxt = halo_recv[0].astype(F32)
        prv = halo_recv[1].astype(F32)
        far_r = jnp.where(left, nxt, pltpu.roll(prv, 64, 1))
        far_i = jnp.where(left, pltpu.roll(nxt, 64, 1), prv)
        src = lane - off
        keep = (src >= 0) & (src < C)
        turn = lax.rem(C - off, C)
        pr = pltpu.roll(jnp.where(keep, own_r, far_r), turn, 1)
        pi = pltpu.roll(jnp.where(keep, own_i, far_i), turn, 1)
        sr = own_r * pr + own_i * pi
        si = own_i * pr - own_r * pi
        out = jnp.zeros((LAGS, C), F32)
        for k, s in enumerate((sr, si)):
            hi, lo = halves(s)
            cols = slice(k * BINS, (k + 1) * BINS)
            out = out + dot(lagt[0, :, cols], hi) + dot(lagt[0, :, cols], lo) + dot(lagt[1, :, cols], hi)
        near_part[o] = out
        near_send[o] = out.astype(BF)
        return 0

    lax.fori_loop(0, 2, near, 0)

    done(a1, rsem, 0, zc_rows)
    a2[...] = dot(perm[...], a1[...]).astype(BF)
    send_xy(a2, wr, 2)
    done(b1, rsem, 1, xy_rows)
    b2[...] = dot(permt[...], b1[...]).astype(BF)
    send_zc(b2, b3, 3)

    lax.fori_loop(2, NOFF, near, 0)

    def near_to(i, k):
        d = lax.rem(x + i, X)
        return pltpu.make_async_remote_copy(
            near_send.at[d], near_recv.at[i - 1], near_sem.at[0], near_sem.at[1],
            device_id=(chan, d), device_id_type=MESH,
        )

    for i in range(1, X):
        near_to(i, 0).start()

    lane_b = iota((C, C), 1)
    row_b = iota((C, C), 0)
    flip = jnp.where(lane_b + row_b == C - 1, 1.0, 0.0).astype(BF)
    picks = []
    for k in range(MAXLB):
        line = jnp.where(count_ref[...] > k, part_ref[k : k + 1, :], -1).astype(F32)
        column = jnp.sum(jnp.where(lane_b == row_b, jnp.broadcast_to(line, (C, C)), 0.0), axis=1, keepdims=True)
        picks.append(jnp.where(column == lane_b.astype(F32), 1.0, 0.0).astype(BF))
    pick = jnp.concatenate(picks, axis=0)

    done(wr, rsem, 2, xy_rows)
    done(b3, rsem, 3, zc_rows)
    wi[...] = dot(perm[...], b3[...]).astype(BF)

    far = []
    own = []
    for s in range(SEGS):
        pair = (wr[s * C : (s + 1) * C, :], wi[s * C : (s + 1) * C, :])
        far.append(tuple(dot(pick, dot(v, flip).astype(BF)) for v in pair))
        own.append(tuple(v.astype(F32) for v in pair))

    def loop_spec(k):
        real, imag = jnp.zeros((C, C), F32), jnp.zeros((C, C), F32)
        for s in range(SEGS):
            own_r, own_i = own[s]
            pr, pi = (v[k * C : (k + 1) * C, :] for v in far[s])
            real = real + own_r * pr + own_i * pi
            imag = imag + own_i * pr - own_r * pi
        return real, imag

    def gather_lanes(parts, q):
        out = jnp.zeros((C, C), F32)
        for j, p in enumerate(parts):
            turned = p if j == q else pltpu.roll(p, 32 * ((j - q) % 4), 1)
            out = jnp.where((lane_b >= 32 * j) & (lane_b < 32 * (j + 1)), turned, out)
        return out.astype(BF)

    done(a2, ssem, 2, xy_rows)
    done(b2, ssem, 3, zc_rows)
    done(white_a, ssem, 0, zc_rows)
    done(white_b, ssem, 1, xy_rows)
    first = loop_spec(0) + loop_spec(1)
    for q in range(X):
        back_a[q * C : (q + 1) * C, :] = gather_lanes(first, q)
    a3[...] = dot(permt[...], back_a[...]).astype(BF)
    send_zc(a3, a4, 4)
    second = loop_spec(2)
    for q in range(X):
        back_b[q * C : (q + 1) * C, :] = gather_lanes(second, q)
    send_xy(back_b, b4, 5)

    three = near_recv.at[pl.ds(0, X - 1)]
    pltpu.make_async_copy(three, three, near_sem.at[1]).wait()
    total = near_part[x]
    for i in range(X - 1):
        total = total + near_recv[i].astype(F32)
    near_out[...] = jnp.transpose(total)

    done(a4, rsem, 4, zc_rows)
    a2[...] = dot(perm[...], a4[...]).astype(BF)
    send_xy(a2, a5, 6)
    done(b4, rsem, 5, xy_rows)
    b2[...] = dot(permt[...], b4[...]).astype(BF)
    send_zc(b2, b5, 7)

    done(a5, rsem, 6, xy_rows)
    got_a = dot(permt[...], a5[...]).astype(BF)
    lag_r = dot(lagt[0, :, :BINS], got_a) + dot(lagt[1, :, :BINS], got_a)
    lag_i = dot(lagt[0, :, BINS:], got_a) + dot(lagt[1, :, BINS:], got_a)
    lag_r = jnp.transpose(lag_r)
    lag_i = jnp.transpose(lag_i)
    loop_out[0] = lag_r[0:32] + lag_i[32:64]
    loop_out[1] = lag_r[64:96] + lag_i[96:128]
    done(b5, rsem, 7, zc_rows)
    got_b = b5[...]
    lag_r = dot(lagt[0, :, :BINS], got_b) + dot(lagt[1, :, :BINS], got_b)
    lag_i = dot(lagt[0, :, BINS:], got_b) + dot(lagt[1, :, BINS:], got_b)
    lag_r = jnp.transpose(lag_r)
    lag_i = jnp.transpose(lag_i)
    loop_out[2] = lag_r[0:32] + lag_i[32:64]

    pltpu.make_async_copy(three, three, near_sem.at[0]).wait()
    done(a3, ssem, 4, zc_rows)
    done(back_b, ssem, 5, xy_rows)
    done(a2, ssem, 6, xy_rows)
    done(b2, ssem, 7, zc_rows)


def write_out(near_ref, loop_ref, near_out, loop_out):
    near_out[:, 0, :] = near_ref[...]
    loop_out[0] = loop_ref[...]


def body(recording, filter_taps, offsets, loop_partner, loop_count):
    fwd = jnp.asarray(forward_tables())
    lagt = jnp.asarray(lag_tables())
    vmem = pl.BlockSpec(memory_space=pltpu.VMEM)
    hbm = pl.BlockSpec(memory_space=pltpu.HBM)
    rows = pltpu.VMEM((BINS, C), BF)
    dma = pltpu.SemaphoreType.DMA
    near, loop = pl.pallas_call(
        kernel,
        out_shape=(
            jax.ShapeDtypeStruct((C, LAGS), F32),
            jax.ShapeDtypeStruct((MAXLB, C // X, LAGS), F32),
        ),
        in_specs=[hbm] * 7,
        out_specs=(vmem, vmem),
        scratch_shapes=[
            pltpu.SMEM((NOFF,), jnp.int32),
            pltpu.VMEM((1, TAPS), F32),
            pltpu.VMEM((MAXLB, C), jnp.int32),
            pltpu.VMEM((1, C), jnp.int32),
            pltpu.VMEM((C, NFFT * DECIM), F32),
            pltpu.VMEM((2 * C, RIM + NFFT * DECIM), BF),
            pltpu.VMEM((NFFT, C), F32),
            pltpu.VMEM((4, BINS, NFFT // 2), BF),
            pltpu.VMEM((2, LAGS, 2 * BINS), BF),
            pltpu.VMEM((BINS, BINS), BF),
            pltpu.VMEM((BINS, BINS), BF),
            pltpu.VMEM((BINS, BINS), BF),
            pltpu.VMEM((C, RIM), BF),
            pltpu.VMEM((C, RIM), BF),
            pltpu.VMEM((2, BINS, C), F32),
            pltpu.VMEM((2, NFFT // 2, 2 * C), BF),
            rows, rows,
            pltpu.VMEM((2, BINS, C), BF),
            pltpu.VMEM((2, BINS, C), BF),
            rows, rows, rows, rows, rows, rows, rows, rows, rows, rows, rows, rows,
            pltpu.VMEM((NOFF, LAGS, C), F32),
            pltpu.VMEM((NOFF, LAGS, C), BF),
            pltpu.VMEM((X - 1, LAGS, C), BF),
            rows, rows,
            dma((NB + 2,)), dma((4,)), dma((2,)), dma((4,)), dma((2,)), dma((8,)), dma((8,)),
        ],
        compiler_params=pltpu.CompilerParams(collective_id=0, has_side_effects=True, vmem_limit_bytes=32 << 20),
    )(*(
        pltpu.with_memory_space_constraint(v, pltpu.HBM)
        for v in (
            offsets, recording, filter_taps.reshape(1, TAPS), loop_partner.T,
            loop_count.reshape(1, C), fwd, lagt,
        )
    ))
    return pl.pallas_call(
        write_out,
        out_shape=(
            jax.ShapeDtypeStruct((C, 1, LAGS), F32),
            jax.ShapeDtypeStruct((1, MAXLB, C // X, LAGS), F32),
        ),
        in_specs=[vmem, vmem],
        out_specs=(vmem, vmem),
        compiler_params=pltpu.CompilerParams(vmem_limit_bytes=4 << 20),
    )(near, loop)


def solution(mesh):
    in_specs = (P("chan", "seg"), P(), P(), P(), P())
    out_specs = (P("chan", "seg", None), P("chan", None, "seg", None))
    return jax.shard_map(body, mesh=mesh, in_specs=in_specs, out_specs=out_specs, check_vma=False)
```

```python
import math

import jax
import jax.numpy as jnp
import numpy as np
from jax import lax
from jax.experimental import pallas as pl
from jax.experimental.pallas import tpu as pltpu
from jax.sharding import PartitionSpec as P

C = 128
NOFF = 4
NFFT = 1024
LAGS = 256
TAPS = 64
DECIM = 4
HALFBAND = 10
BINS = 512
MAXLB = 3
SEGS = 4
WATER = 0.2
X, Y, ZC = 4, 8, 16
XY = X * Y
RIM = 128
QB = 128
WIN = DECIM * QB + RIM
NB = NFFT // QB
MESH = pl.DeviceIdType.MESH
BF = jnp.bfloat16
F32 = jnp.float32


def split_np(a):
    hi = a.astype(np.float32).astype(jnp.bfloat16)
    lo = (a - hi.astype(np.float64)).astype(np.float32).astype(jnp.bfloat16)
    return hi, lo


def bin_order():
    p = np.arange(BINS)
    return np.where(p < BINS // 2, 2 * p, 2 * (p - BINS // 2) + 1)


def forward_tables():
    sample = np.arange(NFFT // 2)
    out = []
    for odd in range(2):
        bins = 2 * np.arange(BINS // 2) + odd
        angle = 2.0 * np.pi * (bins[:, None] * sample[None, :] % NFFT) / NFFT
        real = np.cos(angle) * (bins[:, None] > 0)
        out.extend(split_np(np.concatenate([real, -np.sin(angle)], axis=0)))
    return np.stack(out)


def lag_tables():
    bins = bin_order()
    lag = np.arange(LAGS) - LAGS // 2
    angle = 2.0 * np.pi * (bins[None, :] * lag[:, None] % NFFT) / NFFT
    weight = np.where(bins == 0, 1.0, 2.0) / math.sqrt(2.0 * BINS * SEGS)
    both = np.concatenate([np.cos(angle) * weight, -np.sin(angle) * weight], axis=1)
    return np.stack(split_np(both))


def dot(a, b):
    return jnp.dot(a, b, preferred_element_type=F32)


def dot_nt(a, b):
    return lax.dot_general(a, b, (((1,), (1,)), ((), ())), preferred_element_type=F32)


def halves(a):
    hi = a.astype(BF)
    return hi, (a - hi.astype(F32)).astype(BF)


def iota(shape, dim):
    return lax.broadcasted_iota(jnp.int32, shape, dim)


def wrap(v, n):
    v = jnp.where(v >= n, v - n, v)
    return jnp.where(v < 0, v + n, v)


def where_am_i():
    chan = lax.axis_index("chan")
    return lax.axis_index("seg"), chan // ZC, lax.rem(chan, ZC)


def kernel(
    off_hbm, rec_hbm, taps_hbm, part_hbm, count_hbm, fwd_hbm, lag_hbm,
    near_out, loop_out,
    off_ref, taps_ref, part_ref, count_ref,
    raw, rec, dec, fwd, lagt, lagp, perm, permt, band, rim_send, rim_recv,
    spec, uv, white_a, white_b, halo_send, halo_recv,
    a1, a2, a3, b1, b2, b3, wr, wi, a4, a5, b4, b5, near_part, near_send, near_recv, back_a, back_b,
    local_sem, small_sem, rim_sem, halo_sem, near_sem, ssem, rsem,
):
    x, y, zc = where_am_i()
    chan = lax.axis_index("chan")

    def zc_dev(d):
        return (y * ZC + d, x)

    def xy_dev(x2, y2):
        return (y2 * ZC + zc, x2)

    me_xy = x * Y + y

    xs = [wrap(x + dx, X) for dx in range(X)]

    def each_zc(do):
        do(wrap(zc + ZC // 2, ZC))

        def pair(i, _):
            do(wrap(zc + (ZC // 2 - i), ZC))
            do(wrap(zc - (ZC // 2 - i), ZC))
            return 0

        lax.fori_loop(1, ZC // 2, pair, 0)

    def each_xy(do):
        def row(y2, dxs):
            for dx in dxs:
                do(xs[dx], y2)

        row(wrap(y + Y // 2, Y), (2, 1, 3, 0))

        def pair(i, _):
            row(wrap(y + (Y // 2 - i), Y), (2, 1, 3, 0))
            row(wrap(y - (Y // 2 - i), Y), (2, 1, 3, 0))
            return 0

        lax.fori_loop(1, Y // 2, pair, 0)
        row(y, (2, 1, 3))

    before = (lax.rem(chan + C - 1, C), x)
    after = (lax.rem(chan + 1, C), x)

    loads = []
    order = [NB - 1] + list(range(NB - 1))
    for n, b in enumerate(order):
        cols = pl.ds(b * DECIM * QB, DECIM * QB)
        loads.append(pltpu.make_async_copy(rec_hbm.at[:, cols], raw.at[:, cols], local_sem.at[n]))
    load_fwd = pltpu.make_async_copy(fwd_hbm, fwd, local_sem.at[NB])
    load_lag = pltpu.make_async_copy(lag_hbm, lagt, local_sem.at[NB + 1])
    small = [
        pltpu.make_async_copy(src, dst, small_sem.at[n])
        for n, (src, dst) in enumerate((
            (taps_hbm, taps_ref), (off_hbm, off_ref), (part_hbm, part_ref), (count_hbm, count_ref),
        ))
    ]
    for c in small + loads:
        c.start()
    load_fwd.start()
    load_lag.start()

    barrier = pltpu.get_barrier_semaphore()

    def signal(device):
        pl.semaphore_signal(barrier, inc=1, device_id=device, device_id_type=MESH)

    each_zc(lambda d: signal(zc_dev(d)))
    each_xy(lambda x2, y2: signal(xy_dev(x2, y2)))
    signal(before)
    signal(after)

    r = iota((BINS, BINS), 0)
    c = iota((BINS, BINS), 1)
    perm[...] = jnp.where(c == lax.rem(r, ZC) * XY + r // ZC, 1.0, 0.0).astype(BF)
    permt[...] = jnp.where(c == lax.rem(r, XY) * ZC + r // XY, 1.0, 0.0).astype(BF)
    half = BINS // 2
    fr = jnp.where(r < half, 2 * r, 2 * (r - half) + 1)
    fc = jnp.where(c < half, 2 * c, 2 * (c - half) + 1)
    band[...] = jnp.where(jnp.abs(fr - fc) <= HALFBAND, 1.0, 0.0).astype(BF)

    place = (iota((TAPS, WIN), 1) == 67 + TAPS - iota((TAPS, WIN), 0))
    place = jnp.where(place, 1.0, 0.0).astype(BF)
    small[0].wait()
    t_hi, t_lo = halves(jnp.broadcast_to(taps_ref[...], (8, TAPS)))
    row_hi = jnp.broadcast_to(dot(t_hi, place)[0:1], (QB, WIN))
    row_lo = jnp.broadcast_to(dot(t_lo, place)[0:1], (QB, WIN))
    tab_hi = pltpu.roll(row_hi, 0, 1, stride=DECIM, stride_axis=0).astype(BF)
    tab_lo = pltpu.roll(row_lo, 0, 1, stride=DECIM, stride_axis=0).astype(BF)

    def take(n):
        b = order[n]
        loads[n].wait()
        cols = pl.ds(b * DECIM * QB, DECIM * QB)
        hi, lo = halves(raw[:, cols])
        to = pl.ds(RIM + b * DECIM * QB, DECIM * QB)
        rec[0:C, to] = hi
        rec[C : 2 * C, to] = lo

    def decimate(b):
        win = pl.ds(b * DECIM * QB, WIN)
        both = dot_nt(tab_hi, rec[:, win])
        out = both[:, :C] + both[:, C:] + dot_nt(tab_lo, rec[0:C, win])
        dec[b * QB : (b + 1) * QB, :] = out

    take(0)
    rim_send[...] = raw[:, NFFT * DECIM - RIM :].astype(BF)
    for n in range(1, NB):
        take(n)
        if order[n] > 0:
            decimate(order[n])
    decimate(NB - 1)

    pl.semaphore_wait(barrier, ZC - 1 + XY - 1 + 2)
    rim = pltpu.make_async_remote_copy(
        rim_send, rim_recv, rim_sem.at[0], rim_sem.at[1],
        device_id=(chan, lax.rem(x + 1, X)), device_id_type=MESH,
    )
    rim.start()

    level = jnp.sum(dec[QB:, :], axis=0, keepdims=True) * (1.0 / (NFFT - QB))

    def fold(lo_row, hi_row):
        low = dec[lo_row:hi_row, :] - level
        high = dec[lo_row + NFFT // 2 : hi_row + NFFT // 2, :] - level
        for k, v in enumerate((low + high, low - high)):
            hi, lo = halves(v)
            uv[k, lo_row:hi_row, 0:C] = hi
            uv[k, lo_row:hi_row, C : 2 * C] = lo

    def transform(lo_row, hi_row):
        outs = []
        for k in range(2):
            v = uv[k, lo_row:hi_row, :]
            both = dot(fwd[2 * k, :, lo_row:hi_row], v)
            outs.append(both[:, :C] + both[:, C:] + dot(fwd[2 * k + 1, :, lo_row:hi_row], v[:, :C]))
        return outs

    fold(QB, NFFT // 2)
    load_fwd.wait()
    for k, s in enumerate(transform(QB, NFFT // 2)):
        spec[k] = s

    rim.wait()
    inside = (iota((C, RIM), 1) >= RIM - TAPS) & (x > 0)
    rec[0:C, 0:RIM] = jnp.where(inside, rim_recv[...].astype(F32), 0.0).astype(BF)
    rec[C : 2 * C, 0:RIM] = jnp.zeros((C, RIM), BF)
    decimate(0)
    fold(0, QB)
    for k, s in enumerate(transform(0, QB)):
        spec[k] = spec[k] + s

    real = jnp.concatenate([spec[0, :half, :], spec[1, :half, :]], axis=0)
    imag = jnp.concatenate([spec[0, half:, :], spec[1, half:, :]], axis=0)
    amp = jnp.sqrt(real * real + imag * imag)
    amp_hi, amp_lo = halves(amp)
    near_sum = dot(band[...], amp_hi) + dot(band[...], amp_lo)
    rows = iota((BINS, C), 0)
    f = jnp.where(rows < half, 2 * rows, 2 * (rows - half) + 1)
    width = jnp.minimum(f, HALFBAND) + jnp.minimum(BINS - 1 - f, HALFBAND) + 1
    mean_amp = jnp.sum(amp, axis=0, keepdims=True) * (1.0 / BINS)
    divisor = near_sum / width.astype(F32) + WATER * mean_amp + 1e-06
    wre = (real / divisor).astype(BF)
    wim = (imag / divisor).astype(BF)
    white_a[...] = wre
    white_b[...] = dot(perm[...], wim).astype(BF)

    def send_zc(src, dst, k):
        mine = pl.ds(pl.multiple_of(zc * XY, XY), XY)

        def one(d):
            pltpu.make_async_remote_copy(
                src.at[pl.ds(pl.multiple_of(d * XY, XY), XY)], dst.at[mine], ssem.at[k], rsem.at[k],
                device_id=zc_dev(d), device_id_type=MESH,
            ).start()

        each_zc(one)
        dst[mine, :] = src[mine, :]

    def send_xy(src, dst, k):
        mine = pl.ds(pl.multiple_of(me_xy * ZC, ZC), ZC)

        def one(x2, y2):
            pltpu.make_async_remote_copy(
                src.at[pl.ds(pl.multiple_of((x2 * Y + y2) * ZC, ZC), ZC)], dst.at[mine], ssem.at[k], rsem.at[k],
                device_id=xy_dev(x2, y2), device_id_type=MESH,
            ).start()

        each_xy(one)
        dst[mine, :] = src[mine, :]

    def done(ref, sems, k, count):
        part = ref.at[pl.ds(0, count)]
        pltpu.make_async_copy(part, part, sems.at[k]).wait()

    zc_rows = (ZC - 1) * XY
    xy_rows = (XY - 1) * ZC

    send_zc(white_a, a1, 0)
    send_xy(white_b, b1, 1)

    lane = iota((BINS, C), 1)
    left = lane < 64
    wre = wre.astype(F32)
    wim = wim.astype(F32)
    halo_send[0] = jnp.where(left, wre, pltpu.roll(wim, 64, 1)).astype(BF)
    halo_send[1] = jnp.where(left, pltpu.roll(wre, 64, 1), wim).astype(BF)
    to_before = pltpu.make_async_remote_copy(
        halo_send.at[0], halo_recv.at[0], halo_sem.at[0], halo_sem.at[1],
        device_id=before, device_id_type=MESH,
    )
    to_after = pltpu.make_async_remote_copy(
        halo_send.at[1], halo_recv.at[1], halo_sem.at[2], halo_sem.at[3],
        device_id=after, device_id_type=MESH,
    )
    to_before.start()
    to_after.start()
    def near(o, _):
        off = off_ref[o]
        own_r = white_a[...].astype(F32)
        own_i = wim
        nxt = halo_recv[0].astype(F32)
        prv = halo_recv[1].astype(F32)
        far_r = jnp.where(left, nxt, pltpu.roll(prv, 64, 1))
        far_i = jnp.where(left, pltpu.roll(nxt, 64, 1), prv)
        src = lane - off
        keep = (src >= 0) & (src < C)
        turn = lax.rem(C - off, C)
        pr = pltpu.roll(jnp.where(keep, own_r, far_r), turn, 1)
        pi = pltpu.roll(jnp.where(keep, own_i, far_i), turn, 1)
        sr = own_r * pr + own_i * pi
        si = own_i * pr - own_r * pi
        out = jnp.zeros((LAGS, C), F32)
        for k, s in enumerate((sr, si)):
            hi, lo = halves(s)
            cols = slice(k * BINS, (k + 1) * BINS)
            out = out + dot(lagt[0, :, cols], hi) + dot(lagt[0, :, cols], lo) + dot(lagt[1, :, cols], hi)
        near_part[o] = out
        near_send[o] = out.astype(BF)
        return 0

    done(a1, rsem, 0, zc_rows)
    a2[...] = dot(perm[...], a1[...]).astype(BF)
    send_xy(a2, wr, 2)
    done(b1, rsem, 1, xy_rows)
    b2[...] = dot(permt[...], b1[...]).astype(BF)
    send_zc(b2, b3, 3)

    to_before.wait()
    to_after.wait()
    load_lag.wait()
    for c in small[1:]:
        c.wait()
    lax.fori_loop(0, NOFF, near, 0)

    def near_to(i, k):
        d = lax.rem(x + i, X)
        return pltpu.make_async_remote_copy(
            near_send.at[d], near_recv.at[i - 1], near_sem.at[0], near_sem.at[1],
            device_id=(chan, d), device_id_type=MESH,
        )

    for i in range(1, X):
        near_to(i, 0).start()

    lane_b = iota((C, C), 1)
    row_b = iota((C, C), 0)
    flip = jnp.where(lane_b + row_b == C - 1, 1.0, 0.0).astype(BF)
    picks = []
    for k in range(MAXLB):
        line = jnp.where(count_ref[...] > k, part_ref[k : k + 1, :], -1).astype(F32)
        column = jnp.sum(jnp.where(lane_b == row_b, jnp.broadcast_to(line, (C, C)), 0.0), axis=1, keepdims=True)
        picks.append(jnp.where(column == lane_b.astype(F32), 1.0, 0.0).astype(BF))
    pick = jnp.concatenate(picks, axis=0)

    def pick_far(w):
        parts = [w[s * C : (s + 1) * C, :] for s in range(SEGS)]
        return [v.astype(F32) for v in parts], [dot(pick, dot(v, flip).astype(BF)) for v in parts]

    done(wr, rsem, 2, xy_rows)
    own_re, far_re = pick_far(wr)
    done(b3, rsem, 3, zc_rows)
    wi[...] = dot(perm[...], b3[...]).astype(BF)
    own_im, far_im = pick_far(wi)

    def loop_spec(k):
        real, imag = jnp.zeros((C, C), F32), jnp.zeros((C, C), F32)
        for s in range(SEGS):
            own_r, own_i = own_re[s], own_im[s]
            pr, pi = (v[s][k * C : (k + 1) * C, :] for v in (far_re, far_im))
            real = real + own_r * pr + own_i * pi
            imag = imag + own_i * pr - own_r * pi
        return real, imag

    def gather_lanes(parts, q):
        out = jnp.zeros((C, C), F32)
        for j, p in enumerate(parts):
            turned = p if j == q else pltpu.roll(p, 32 * ((j - q) % 4), 1)
            out = jnp.where((lane_b >= 32 * j) & (lane_b < 32 * (j + 1)), turned, out)
        return out.astype(BF)

    done(a2, ssem, 2, xy_rows)
    done(b2, ssem, 3, zc_rows)
    done(white_a, ssem, 0, zc_rows)
    done(white_b, ssem, 1, xy_rows)
    first = loop_spec(0) + loop_spec(1)
    for q in range(X):
        back_a[q * C : (q + 1) * C, :] = gather_lanes(first, q)
    a3[...] = dot(permt[...], back_a[...]).astype(BF)
    send_zc(a3, a4, 4)
    second = loop_spec(2)
    for q in range(X):
        back_b[q * C : (q + 1) * C, :] = gather_lanes(second, q)
    send_xy(back_b, b4, 5)

    three = near_recv.at[pl.ds(0, X - 1)]
    pltpu.make_async_copy(three, three, near_sem.at[1]).wait()
    total = near_part[x]
    for i in range(X - 1):
        total = total + near_recv[i].astype(F32)
    near_out[...] = jnp.transpose(total)
    for n in range(2):
        for k in range(2):
            lagp[n, :, k * BINS : (k + 1) * BINS] = dot(lagt[n, :, k * BINS : (k + 1) * BINS], permt[...]).astype(BF)

    done(a4, rsem, 4, zc_rows)
    a2[...] = dot(perm[...], a4[...]).astype(BF)
    send_xy(a2, a5, 6)
    done(b4, rsem, 5, xy_rows)
    b2[...] = dot(permt[...], b4[...]).astype(BF)
    send_zc(b2, b5, 7)

    done(a5, rsem, 6, xy_rows)
    def lags(table, got):
        real = dot(table[0, :, :BINS], got) + dot(table[1, :, :BINS], got)
        imag = dot(table[0, :, BINS:], got) + dot(table[1, :, BINS:], got)
        return real + pltpu.roll(imag, C - 32, 1)

    lag_a = lags(lagp, a5[...])
    done(b5, rsem, 7, zc_rows)
    lag_b = pltpu.roll(lags(lagt, b5[...]), 32, 1)
    lane_l = iota((LAGS, C), 1)
    both = jnp.transpose(jnp.where((lane_l >= 32) & (lane_l < 64), lag_b, lag_a))
    loop_out[0] = both[0:32]
    loop_out[1] = both[64:96]
    loop_out[2] = both[32:64]

    pltpu.make_async_copy(three, three, near_sem.at[0]).wait()
    done(a3, ssem, 4, zc_rows)
    done(back_b, ssem, 5, xy_rows)
    done(a2, ssem, 6, xy_rows)
    done(b2, ssem, 7, zc_rows)


def write_out(near_ref, loop_ref, near_out, loop_out):
    near_out[:, 0, :] = near_ref[...]
    loop_out[0] = loop_ref[...]


def body(recording, filter_taps, offsets, loop_partner, loop_count):
    fwd = jnp.asarray(forward_tables())
    lagt = jnp.asarray(lag_tables())
    vmem = pl.BlockSpec(memory_space=pltpu.VMEM)
    hbm = pl.BlockSpec(memory_space=pltpu.HBM)
    rows = pltpu.VMEM((BINS, C), BF)
    dma = pltpu.SemaphoreType.DMA
    near, loop = pl.pallas_call(
        kernel,
        out_shape=(
            jax.ShapeDtypeStruct((C, LAGS), F32),
            jax.ShapeDtypeStruct((MAXLB, C // X, LAGS), F32),
        ),
        in_specs=[hbm] * 7,
        out_specs=(vmem, vmem),
        scratch_shapes=[
            pltpu.SMEM((NOFF,), jnp.int32),
            pltpu.VMEM((1, TAPS), F32),
            pltpu.VMEM((MAXLB, C), jnp.int32),
            pltpu.VMEM((1, C), jnp.int32),
            pltpu.VMEM((C, NFFT * DECIM), F32),
            pltpu.VMEM((2 * C, RIM + NFFT * DECIM), BF),
            pltpu.VMEM((NFFT, C), F32),
            pltpu.VMEM((4, BINS, NFFT // 2), BF),
            pltpu.VMEM((2, LAGS, 2 * BINS), BF),
            pltpu.VMEM((2, LAGS, 2 * BINS), BF),
            pltpu.VMEM((BINS, BINS), BF),
            pltpu.VMEM((BINS, BINS), BF),
            pltpu.VMEM((BINS, BINS), BF),
            pltpu.VMEM((C, RIM), BF),
            pltpu.VMEM((C, RIM), BF),
            pltpu.VMEM((2, BINS, C), F32),
            pltpu.VMEM((2, NFFT // 2, 2 * C), BF),
            rows, rows,
            pltpu.VMEM((2, BINS, C), BF),
            pltpu.VMEM((2, BINS, C), BF),
            rows, rows, rows, rows, rows, rows, rows, rows, rows, rows, rows, rows,
            pltpu.VMEM((NOFF, LAGS, C), F32),
            pltpu.VMEM((NOFF, LAGS, C), BF),
            pltpu.VMEM((X - 1, LAGS, C), BF),
            rows, rows,
            dma((NB + 2,)), dma((4,)), dma((2,)), dma((4,)), dma((2,)), dma((8,)), dma((8,)),
        ],
        compiler_params=pltpu.CompilerParams(collective_id=0, has_side_effects=True, vmem_limit_bytes=32 << 20),
    )(*(
        pltpu.with_memory_space_constraint(v, pltpu.HBM)
        for v in (
            offsets, recording, filter_taps.reshape(1, TAPS), loop_partner.T,
            loop_count.reshape(1, C), fwd, lagt,
        )
    ))
    return pl.pallas_call(
        write_out,
        out_shape=(
            jax.ShapeDtypeStruct((C, 1, LAGS), F32),
            jax.ShapeDtypeStruct((1, MAXLB, C // X, LAGS), F32),
        ),
        in_specs=[vmem, vmem],
        out_specs=(vmem, vmem),
        compiler_params=pltpu.CompilerParams(vmem_limit_bytes=4 << 20),
    )(near, loop)


def solution(mesh):
    in_specs = (P("chan", "seg"), P(), P(), P(), P())
    out_specs = (P("chan", "seg", None), P("chan", None, "seg", None))
    return jax.shard_map(body, mesh=mesh, in_specs=in_specs, out_specs=out_specs, check_vma=False)
```
